32 devices in a mesh: rows: 4 (over z), cols: 8 (over y, x, core).
Axes of the slice: x: 2, y: 2, z: 4, core: 2. Of those that a mesh axis runs over, the one named last changes fastest.
Arguments:
- left_fine: bfloat16 [128, 1024, 128], P('rows', 'cols'), may hold values from -40 to 40
- right_fine: bfloat16 [128, 1024, 128], P('rows', 'cols'), may hold values from -40 to 40
- left_coarse: bfloat16 [32, 256, 128], P('rows', 'cols'), may hold values from -40 to 40
- right_coarse: bfloat16 [32, 256, 128], P('rows', 'cols'), may hold values from -40 to 40
- candidates: int32 [8, 32, 4], P(None, 'rows'), may hold values from 0 to 7, all different within a row; in each aligned block of 8 rows (0 to 7, 8 to 15, ..., all dimensions but the last counted through in order) at most 8 rows name the same one
- counts: int32 [8, 32], P(None, 'rows'), may hold values from 1 to 4
- query_weight: bfloat16 [128, 128], replicated, may hold values from -1 to 1
- key_weight: bfloat16 [128, 128], replicated, may hold values from -1 to 1
- value_weight: bfloat16 [128, 128], replicated, may hold values from -0.5 to 0.5
- out_weight: bfloat16 [128, 128], replicated, may hold values from -0.5 to 0.5
- norm_gain: float32 [128], replicated, may hold values from 0.5 to 1.5
Outputs:
- fine_features: bfloat16 [128, 1024, 128], P('rows', 'cols')
- coarse_prior: bfloat16 [32, 256, 128], P('rows', 'cols')
The draws below stay inside these ranges and needn't reach their ends.
Inputs may be any that keep to these rules, and one draw needn't show every extreme that they name: `candidates`: each list names 4 different right blocks; entries at k >= counts are not used. For one left block, within the 8 bands of one index of rows (aligned groups of bands), no right block is named more than 8 times, and in some groups one is named exactly 8 times.
All inputs are finite; a program needn't handle non-finite values.
Results may differ from the reference program's by a relative error of at most 0.01.
Values may be sent and summed in bfloat16 or wider, within the bound.
A program may use at most 192 MiB of HBM per device.

```python
import math
import jax
import jax.numpy as jnp
import numpy as np
from jax import lax

FEAT = 128
HEADS = 8
HEAD_DIM = 16
BLOCK = 128
BAND = 4
CANDS = 4
BANDS_DEV = 8
ROWS_FINE = 128
COLS_FINE = 1024
ROWS_COARSE = 32
COLS_COARSE = 256
BANDS = 32
CAP = 8
N_COLS = 8


def background(key, salt, shape):
    values = jnp.clip(jax.random.normal(jax.random.fold_in(key, salt), shape, jnp.float32), -4.0, 4.0)
    return values


def draw_left_fine(key, part):
    values = background(key, 31, (ROWS_FINE, COLS_FINE, FEAT))
    return values.astype(jnp.bfloat16)


def draw_right_fine(key, part):
    values = background(key, 33, (ROWS_FINE, COLS_FINE, FEAT))
    return values.astype(jnp.bfloat16)


def draw_left_coarse(key, part):
    values = background(key, 35, (ROWS_COARSE, COLS_COARSE, FEAT))
    return values.astype(jnp.bfloat16)


def draw_right_coarse(key, part):
    values = background(key, 37, (ROWS_COARSE, COLS_COARSE, FEAT))
    return values.astype(jnp.bfloat16)


def weight_base(key, salt):
    values = jnp.clip(jax.random.normal(jax.random.fold_in(key, salt), (FEAT, FEAT), jnp.float32), -4.0, 4.0)
    return values / jnp.sqrt(jnp.float32(FEAT))


def draw_query_weight(key, part):
    return weight_base(key, 51).astype(jnp.bfloat16)


def draw_key_weight(key, part):
    jitter = weight_base(key, 52)
    values = jitter
    return values.astype(jnp.bfloat16)


def with_ends(entries, stream_key, low, high):
    dims = entries.shape
    place = [jax.random.randint(jax.random.fold_in(stream_key, axis), (), 0, dims[axis]) for axis in range(len(dims))]
    entries = entries.at[tuple(place)].set(low)
    longest = dims.index(max(dims))
    place[longest] = (place[longest] + 1) % dims[longest]
    return entries.at[tuple(place)].set(high)


def shared_out(own_key, own, number, rows, number_of, top, reach, lean):
    order = jax.random.permutation(own_key, number_of)
    packed, common = portions_of(number_of, rows * top, reach, lean, True), portions_of(number_of, rows * top, reach, lean, False)
    places = jnp.arange(number_of)

    def named(tallies, rotation):
        used = int((tallies > 0).sum())
        fixed = max(1, used // 4)
        passed = fixed + (places - fixed + rotation * (used - fixed)) % max(1, number_of - fixed)
        return jnp.zeros((number_of,), jnp.int32).at[order[jnp.where(places < fixed, places, passed)]].set(jnp.asarray(tallies, jnp.int32))

    tallies = jnp.where(number % 4 == 0, named(packed, number // 4), named(common, number - number // 4 - 1))
    mixed = jax.random.permutation(jax.random.fold_in(own, 3), number_of)
    giver, receiver = mixed[0:number_of // 2 * 2:2], mixed[1:number_of // 2 * 2:2]
    room = jnp.minimum(tallies[giver] - 1, reach - tallies[receiver]) // 2
    room = jnp.where((giver == order[0]) | (receiver == order[0]) | (tallies[receiver] == 0), 0, jnp.maximum(room, 0))
    passed = jax.random.randint(jax.random.fold_in(own, 4), (number_of // 2,), 0, 1 << 20) % (room + 1)
    tallies = tallies.at[giver].add(-passed).at[receiver].add(passed)
    labels = jnp.searchsorted(jnp.cumsum(tallies), jnp.arange(rows * top), side="right").astype(jnp.int32)
    table = labels.reshape(top, rows).T
    table = table[jax.random.permutation(jax.random.fold_in(own, 1), rows)]
    rotation = jax.random.randint(jax.random.fold_in(own, 2), (rows, 1), 0, top)
    return jnp.take_along_axis(table, (jnp.arange(top)[None, :] + rotation) % top, axis=1)


def portions_of(amount, total, limit, skew, full):
    weights = [(1 << 20) // math.isqrt(grade ** skew) + 1 for grade in range(1, amount + 1)]
    largest = limit if full else min(limit, max(-(-total // amount), total * weights[0] // sum(weights)))
    least = 1 if total - largest >= amount - 1 else 0
    given, surplus = [largest] + [least] * (amount - 1), total - largest - least * (amount - 1)
    while surplus > 0:
        free = [i for i in range(1, amount) if given[i] < largest] or [i for i in range(1, amount) if given[i] < limit]
        pool, remaining = sum([weights[i] for i in free]), surplus
        for i in free:
            extra = min(limit - given[i], max(1, remaining * weights[i] // pool), surplus)
            given[i] = given[i] + extra
            surplus = surplus - extra
    return np.array(given)


def gaussian(own_key, extent, scale, reach, kind=jnp.bfloat16):
    result = jax.random.normal(own_key, extent, jnp.float32) * scale
    return jnp.minimum(jnp.maximum(result, -reach), reach).astype(kind)


def setup_inputs(seed: int = 0) -> dict:
    seeds = jax.random.split(jax.random.key(seed), 12)
    left_fine = draw_left_fine(jax.random.fold_in(seeds[11], 71), 0)
    right_fine = draw_right_fine(jax.random.fold_in(seeds[11], 71), 0)
    left_coarse = draw_left_coarse(jax.random.fold_in(seeds[11], 71), 0)
    right_coarse = draw_right_coarse(jax.random.fold_in(seeds[11], 71), 0)
    candidates_keys = jax.random.split(jax.random.fold_in(seeds[4], 1), N_COLS * BANDS // BANDS_DEV)
    candidates_turns = jax.random.permutation(jax.random.fold_in(seeds[4], 3), N_COLS * BANDS // BANDS_DEV)
    candidates = jax.vmap(lambda own, number: shared_out(jax.random.fold_in(seeds[4], 2), own, number, BANDS_DEV, N_COLS, CANDS, CAP, 2))(candidates_keys, candidates_turns).reshape((N_COLS, BANDS, CANDS))
    counts = with_ends(jax.random.randint(seeds[5], (N_COLS, BANDS), 1, CANDS + 1), jax.random.fold_in(seeds[5], 1), 1, CANDS).astype(jnp.int32)
    query_weight = draw_query_weight(jax.random.fold_in(seeds[11], 71), 0)
    key_weight = draw_key_weight(jax.random.fold_in(seeds[11], 71), 0)
    value_weight = gaussian(seeds[8], (FEAT, FEAT), FEAT ** -0.5, 0.5)
    out_weight = gaussian(seeds[9], (FEAT, FEAT), FEAT ** -0.5, 0.5)
    norm_gain = jnp.clip(1.0 + 0.1 * jax.random.normal(seeds[10], (FEAT,), jnp.float32), 0.5, 1.5)
    return {"left_fine": left_fine, "right_fine": right_fine, "left_coarse": left_coarse, "right_coarse": right_coarse, "candidates": candidates, "counts": counts, "query_weight": query_weight, "key_weight": key_weight, "value_weight": value_weight, "out_weight": out_weight, "norm_gain": norm_gain}


EPSILON = 1e-05

def layer_norm(values, norm_gain):
    average = lax.optimization_barrier(jnp.mean(values, axis=-1, keepdims=True))
    centred = values - average
    spread = lax.optimization_barrier(jnp.mean(centred * centred, axis=-1, keepdims=True))
    return centred * lax.rsqrt(spread + EPSILON) * norm_gain

def project(values, weight):
    flat_rows = values.reshape(-1, values.shape[-1])
    product = jnp.dot(flat_rows, weight, preferred_element_type=jnp.float32)
    return product.astype(jnp.bfloat16).reshape(values.shape[:-1] + (weight.shape[1],))

def split_heads(values):
    return values.reshape(values.shape[:-1] + (HEADS, HEAD_DIM)).astype(jnp.float32)

def blend(values, axis_pos, before_rows, after_rows):
    stacked = jnp.stack([0.375 * before_rows + 0.625 * values, 0.125 * before_rows + 0.875 * values, 0.875 * values + 0.125 * after_rows, 0.625 * values + 0.375 * after_rows], axis=axis_pos + 1)
    new_shape = values.shape[:axis_pos] + (4 * values.shape[axis_pos],) + values.shape[axis_pos + 1:]
    return stacked.reshape(new_shape)

def reference(left_fine, right_fine, left_coarse, right_coarse, candidates, counts, query_weight, key_weight, value_weight, out_weight, norm_gain):
    scale_factor = 1.0 / math.sqrt(HEAD_DIM)
    coarse_query = project(left_coarse, query_weight)
    coarse_key = project(right_coarse, key_weight)
    coarse_value = project(right_coarse, value_weight)

    def coarse_row(inputs):
        row_query, row_key, row_value = inputs
        scores = jnp.einsum('qhd,khd->hqk', split_heads(row_query), split_heads(row_key)) * scale_factor
        weights = jax.nn.softmax(scores, axis=-1).astype(jnp.bfloat16)
        mixture = jnp.einsum('hqk,khd->qhd', weights.astype(jnp.float32), split_heads(row_value))
        return mixture.astype(jnp.bfloat16).reshape(row_query.shape)
    coarse_attn = lax.map(coarse_row, (coarse_query, coarse_key, coarse_value))
    coarse_mix = jnp.dot(coarse_attn.reshape(-1, FEAT), out_weight, preferred_element_type=jnp.float32)
    coarse_mix = coarse_mix.reshape(left_coarse.shape)
    coarse_prior = layer_norm(left_coarse.astype(jnp.float32) + coarse_mix, norm_gain).astype(jnp.bfloat16)
    prior_float = coarse_prior.astype(jnp.float32)

    def fine_band(inputs):
        band_index, left_rows, right_rows, band_cands, band_counts = inputs
        middle_row = lax.dynamic_index_in_dim(prior_float, band_index, 0, keepdims=True)
        lower_row = lax.dynamic_index_in_dim(prior_float, jnp.maximum(band_index - 1, 0), 0, keepdims=True)
        upper_row = lax.dynamic_index_in_dim(prior_float, jnp.minimum(band_index + 1, ROWS_COARSE - 1), 0, keepdims=True)
        row_up = blend(middle_row, 0, lower_row, upper_row)
        left_cols = jnp.concatenate([row_up[:, :1], row_up[:, :-1]], axis=1)
        right_cols = jnp.concatenate([row_up[:, 1:], row_up[:, -1:]], axis=1)
        upsampled = blend(row_up, 1, left_cols, right_cols)
        query_in = (left_rows.astype(jnp.float32) + upsampled).astype(jnp.bfloat16)
        queries = project(query_in, query_weight).reshape(BAND, N_COLS, BLOCK, FEAT)
        keys_band = project(right_rows, key_weight).reshape(BAND, N_COLS, BLOCK, FEAT)
        values_band = project(right_rows, value_weight).reshape(BAND, N_COLS, BLOCK, FEAT)
        picked_keys = keys_band[:, band_cands]
        picked_values = values_band[:, band_cands]
        scores = jnp.einsum('rbqhd,rbckhd->brhqck', split_heads(queries), split_heads(picked_keys)) * scale_factor
        usable = jnp.arange(CANDS, dtype=jnp.int32)[None, :] < band_counts[:, None]
        scores = jnp.where(usable[:, None, None, None, :, None], scores, -1e+30)
        flat_scores = scores.reshape(scores.shape[:4] + (CANDS * BLOCK,))
        weights = jax.nn.softmax(flat_scores, axis=-1).astype(jnp.bfloat16).reshape(scores.shape)
        mixture = jnp.einsum('brhqck,rbckhd->rbqhd', weights.astype(jnp.float32), split_heads(picked_values))
        mixture = mixture.astype(jnp.bfloat16).reshape(BAND * COLS_FINE, FEAT)
        fine_mix = jnp.dot(mixture, out_weight, preferred_element_type=jnp.float32).reshape(BAND, COLS_FINE, FEAT)
        return layer_norm(query_in.astype(jnp.float32) + fine_mix, norm_gain).astype(jnp.bfloat16)
    band_ids = jnp.arange(BANDS, dtype=jnp.int32)
    fine_out = lax.map(fine_band, (band_ids, left_fine.reshape(BANDS, BAND, COLS_FINE, FEAT), right_fine.reshape(BANDS, BAND, COLS_FINE, FEAT), jnp.transpose(candidates, (1, 0, 2)), jnp.transpose(counts, (1, 0))))
    return (fine_out.reshape(ROWS_FINE, COLS_FINE, FEAT), coarse_prior)
```

```python
import functools
import math

import jax
import jax.numpy as jnp
import numpy as np
from jax import lax
from jax.experimental import pallas as pl
from jax.experimental.pallas import tpu as pltpu
from jax.sharding import PartitionSpec as P

HEADS = 8
HEAD_DIM = 16
BLOCK = 128
BAND = 4
EPSILON = 1e-05
PAIRS = HEADS // 2
EDGE = 16
LEAD = 2
MESH = pl.DeviceIdType.MESH
KEY_SCALE = math.log2(math.e) / math.sqrt(HEAD_DIM)
BF16 = jnp.bfloat16
F32 = jnp.float32


def nt(a, b):
    return lax.dot_general(a, b, (((1,), (1,)), ((), ())), preferred_element_type=F32)


def tn(a, b):
    return lax.dot_general(a, b, (((0,), (0,)), ((), ())), preferred_element_type=F32)


def nn(a, b):
    return jnp.dot(a, b, preferred_element_type=F32)


def layer_norm(values, norm_gain):
    average = jnp.mean(values, axis=-1, keepdims=True)
    centred = values - average
    spread = jnp.mean(centred * centred, axis=-1, keepdims=True)
    return centred * lax.rsqrt(spread + EPSILON) * norm_gain


def upsample_matrix(cols):
    taps = np.array(
        [[0.375, 0.625, 0.0], [0.125, 0.875, 0.0], [0.0, 0.875, 0.125], [0.0, 0.625, 0.375]]
    )
    pitch = cols + 2 * EDGE
    out = np.zeros((BAND, cols, 4, 3, pitch), np.float32)
    for c in range(cols):
        for t in range(4):
            for d in range(3):
                out[:, c, t, :, c + d + EDGE - 1] = taps[:, :] * taps[t, d]
    return out.reshape(BAND * cols * 4, 3 * pitch)


def project_row(blocks, wk, wv_t):
    block = jnp.concatenate(blocks, axis=0)
    keys = (nn(block, wk) * KEY_SCALE).astype(BF16)
    return keys, nt(wv_t, block).astype(BF16)


def mix_pair(weights, rows, ones):
    width = weights.shape[1] // 2
    mix = nn(jnp.concatenate([rows, ones], axis=0), weights)
    inverse = 1.0 / mix[2 * HEAD_DIM : 2 * HEAD_DIM + 1]
    return [
        mix[:HEAD_DIM, :width] * inverse[:, :width],
        mix[HEAD_DIM : 2 * HEAD_DIM, width:] * inverse[:, width:],
    ]


def query_stage(left, coarse, up_ref, wq_ref):
    up = nn(up_ref[...], coarse)
    query_in = (left.reshape(up.shape).astype(F32) + up).astype(BF16)
    return query_in, nt(wq_ref[...], query_in).astype(BF16)


def spread_queries(query_ref, spread_ref, start):
    for h in range(HEADS):
        rows = slice(h * HEAD_DIM, (h + 1) * HEAD_DIM)
        spread_ref[rows, h * BLOCK : (h + 1) * BLOCK] = query_ref[rows, pl.ds(start, BLOCK)]


def out_stage(query_in, mixed, wo_ref, gain_ref):
    product = tn(mixed, wo_ref[...])
    return layer_norm(query_in.astype(F32) + product, gain_ref[...]).astype(BF16)


def flipped(index, bit):
    return index + bit - 2 * bit * ((index // bit) % 2)


def gather_hops(n, me):
    if n != 8:
        return [(me, (me + j) % n, (me + n - j) % n, None) for j in range(1, n)]
    a, b, c = flipped(me, 1), flipped(me, 2), flipped(me, 4)
    d = flipped(b, 4)
    odd = me % 2
    relay_block = b + odd * (c - b)
    relay_target = c + odd * (b - c)
    return [
        (me, b, b, None),
        (me, c, c, None),
        (me, a, a, None),
        (relay_block, relay_target, d, (0, 1)),
        (b, a, flipped(b, 1), (0,)),
        (c, a, flipped(c, 1), (1,)),
        (d, a, flipped(d, 1), (3,)),
    ]


def gather_kernel(
    list_ref,
    count_ref,
    left_ref,
    right_ref,
    left_coarse_ref,
    right_coarse_ref,
    up_ref,
    wq_in_ref,
    wk_ref,
    wv_ref,
    wo_ref,
    gain_ref,
    fold_ref,
    fine_ref,
    prior_ref,
    *scratch,
    n,
    row_devices,
):
    bands = right_ref.shape[0] // BAND
    length = list_ref.shape[2]
    bands_ref = scratch[:bands]
    (
        ext_ref,
        wq_ref,
        wv_t_ref,
        score_low_ref,
        score_high_ref,
        top_ref,
        key_ref,
        value_ref,
        input_ref,
        coarse_ref,
        edge_low_ref,
        edge_high_ref,
        rows_ref,
        query_ref,
        spread_ref,
        mix_ref,
        coarse_send,
        coarse_recv,
        edge_send,
        edge_recv,
        fine_send,
        fine_recv,
        local_sem,
    ) = scratch[bands:]
    me = lax.axis_index("cols")
    row = lax.axis_index("rows")
    coarse_rows, coarse_cols, feat = left_coarse_ref.shape
    hops = gather_hops(n, me)

    barrier = pltpu.get_barrier_semaphore()
    for j in range(1, n):
        pl.semaphore_signal(
            barrier, inc=1, device_id={"cols": (me + j) % n}, device_id_type=MESH
        )

    @pl.when(row > 0)
    def _():
        pl.semaphore_signal(barrier, inc=1, device_id={"rows": row - 1}, device_id_type=MESH)

    @pl.when(row < row_devices - 1)
    def _():
        pl.semaphore_signal(barrier, inc=1, device_id={"rows": row + 1}, device_id_type=MESH)

    inner = (row > 0).astype(jnp.int32) + (row < row_devices - 1).astype(jnp.int32)
    pl.semaphore_wait(barrier, n - 1 + inner)

    def coarse_copy(j):
        return pltpu.make_async_remote_copy(
            src_ref=right_coarse_ref,
            dst_ref=coarse_ref.at[me],
            send_sem=coarse_send.at[j - 1],
            recv_sem=coarse_recv.at[j - 1],
            device_id={"cols": (me + j) % n},
            device_id_type=MESH,
        )

    def place(g, block):
        return bands_ref[g].at[block]

    def fine_copy(g, hop):
        block, target, _, after = hops[hop]
        if after is None:
            source = right_ref.at[pl.ds(g * BAND, BAND)]
        else:
            source = place(g, block)
        return pltpu.make_async_remote_copy(
            src_ref=source,
            dst_ref=place(g, block),
            send_sem=fine_send.at[g, hop],
            recv_sem=fine_recv.at[g, hop],
            device_id={"cols": target},
            device_id_type=MESH,
        )

    def own_copy(g):
        return pltpu.make_async_copy(
            right_ref.at[pl.ds(g * BAND, BAND)], place(g, me), local_sem.at[g]
        )

    arrived = [set() for _ in range(bands)]

    def take(g, hop):
        if hop not in arrived[g]:
            arrived[g].add(hop)
            fine_copy(g, hop).wait_recv()

    levels = []
    for hop in hops:
        levels.append(0 if hop[3] is None else 1 + max(levels[i] for i in hop[3]))
    depth = max(levels)

    def send(g, level):
        for hop in range(len(hops)):
            if levels[hop] == level:
                for needed in hops[hop][3] or ():
                    take(g, needed)
                fine_copy(g, hop).start()

    sent = set()

    def tick(*steps):
        for g, level in steps:
            if g < bands and level <= depth and (g, level) not in sent:
                sent.add((g, level))
                send(g, level)

    for j in range(1, n):
        coarse_copy(j).start()
    for g in range(bands):
        own_copy(g).start()
    for g in range(LEAD):
        tick((g, 0))

    spread_ref[...] = jnp.zeros_like(spread_ref)
    wq_ref[...] = wq_in_ref[...].T
    wv_t_ref[...] = wv_ref[...].T
    coarse_ref[me] = right_coarse_ref[...]
    for j in range(1, n):
        coarse_copy(j).wait()

    wide = HEADS * coarse_cols
    diagonal = (
        lax.broadcasted_iota(jnp.int32, (feat, wide), 0) // HEAD_DIM
        == lax.broadcasted_iota(jnp.int32, (feat, wide), 1) // coarse_cols
    )

    def coarse_row(r, carry):
        right = coarse_ref[:, r].reshape(n * coarse_cols, feat)
        left = left_coarse_ref[r]
        keys, values = project_row([right], wk_ref[...], wv_t_ref[...])
        queries = nt(wq_ref[...], jnp.concatenate([left] * HEADS, axis=0))
        queries = jnp.where(diagonal, queries, 0.0).astype(BF16)
        scores = nn(keys, queries)
        top = jnp.max(scores, axis=0, keepdims=True)
        weights = jnp.exp2((scores - top).astype(BF16))
        total = jnp.sum(weights.astype(F32), axis=0, keepdims=True)
        mixed = nn(values, weights) * (1.0 / total)
        mixed = jnp.where(diagonal, mixed, 0.0).astype(BF16)
        folded = nt(fold_ref[...], mixed).astype(BF16)
        out = left.astype(F32) + nn(folded, wo_ref[...])
        out = layer_norm(out, gain_ref[...]).astype(BF16)
        rows_ref[r + 1] = out
        prior_ref[r] = out
        return carry

    lax.fori_loop(0, coarse_rows, coarse_row, 0)
    tick((0, 1))

    def row_copy(up):
        return pltpu.make_async_remote_copy(
            src_ref=prior_ref.at[0 if up else coarse_rows - 1],
            dst_ref=rows_ref.at[coarse_rows + 1 if up else 0],
            send_sem=edge_send.at[0 if up else 1],
            recv_sem=edge_recv.at[0 if up else 1],
            device_id={"rows": row - 1 if up else row + 1},
            device_id_type=MESH,
        )

    def col_copy(left):
        return pltpu.make_async_remote_copy(
            src_ref=rows_ref.at[:, pl.ds(0 if left else coarse_cols - EDGE, EDGE)],
            dst_ref=edge_high_ref if left else edge_low_ref,
            send_sem=edge_send.at[2 if left else 3],
            recv_sem=edge_recv.at[2 if left else 3],
            device_id={"cols": me - 1 if left else me + 1},
            device_id_type=MESH,
        )

    has = (row > 0, row < row_devices - 1, me > 0, me < n - 1)

    @pl.when(has[0])
    def _():
        row_copy(True).start()

    @pl.when(has[1])
    def _():
        row_copy(False).start()

    @pl.when(has[0])
    def _():
        row_copy(False).wait_recv()
        row_copy(True).wait_send()

    @pl.when(jnp.logical_not(has[0]))
    def _():
        rows_ref[0] = rows_ref[1]

    @pl.when(has[1])
    def _():
        row_copy(True).wait_recv()
        row_copy(False).wait_send()

    @pl.when(jnp.logical_not(has[1]))
    def _():
        rows_ref[coarse_rows + 1] = rows_ref[coarse_rows]

    @pl.when(has[2])
    def _():
        col_copy(True).start()

    @pl.when(has[3])
    def _():
        col_copy(False).start()

    tick((LEAD, 0), (1, 1), (LEAD + 1, 0))

    @pl.when(has[2])
    def _():
        col_copy(False).wait_recv()
        col_copy(True).wait_send()

    @pl.when(jnp.logical_not(has[2]))
    def _():
        edge_low_ref[...] = jnp.broadcast_to(rows_ref[:, 0:1], edge_low_ref.shape)

    @pl.when(has[3])
    def _():
        col_copy(True).wait_recv()
        col_copy(False).wait_send()

    @pl.when(jnp.logical_not(has[3]))
    def _():
        edge_high_ref[...] = jnp.broadcast_to(
            rows_ref[:, coarse_cols - 1 : coarse_cols], edge_high_ref.shape
        )

    ext_ref[:, :EDGE] = edge_low_ref[...]
    ext_ref[:, EDGE : EDGE + coarse_cols] = rows_ref[...]
    ext_ref[:, EDGE + coarse_cols :] = edge_high_ref[...]

    tick((0, 2))
    scores_ref = (score_low_ref, score_high_ref)

    def arrive(g):
        own_copy(g).wait()
        for hop in range(len(hops)):
            take(g, hop)

    def queries_of(g):
        coarse = jnp.concatenate([ext_ref[g + i] for i in range(3)], axis=0)
        query_in, queries = query_stage(left_ref[g * BAND : (g + 1) * BAND], coarse, up_ref, wq_ref)
        query_ref[g % 2] = queries
        input_ref[g % 2] = query_in

    def picked(g):
        used = count_ref[me, g]
        picks = [
            jnp.where(k < used, list_ref[me, g, k], list_ref[me, g, 0]) for k in range(length)
        ]
        lanes = lax.broadcasted_iota(jnp.int32, (1, length * BLOCK), 1)
        return picks, jnp.where(lanes < used * BLOCK, 1.0, 0.0).astype(BF16)

    def score(pair):
        scores = nn(key_ref[...], spread_ref[:, pair * 2 * BLOCK : (pair + 1) * 2 * BLOCK])
        scores_ref[pair % 2][...] = scores
        top = jnp.max(scores, axis=0, keepdims=True)
        top_ref[pair % 2] = jnp.broadcast_to(top, top_ref.shape[1:])

    def weigh(pair):
        return jnp.exp2((scores_ref[pair % 2][...] - top_ref[pair % 2][0:1]).astype(BF16))

    def open_row(g, r, picks, live):
        keys, values = project_row(
            [bands_ref[g][picks[k], r] for k in range(length)], wk_ref[...], wv_t_ref[...]
        )
        key_ref[...] = keys
        value_ref[...] = values * live
        start = pl.multiple_of(r * BLOCK, BLOCK)
        spread_queries(query_ref.at[g % 2], spread_ref, start)
        score(0)

    def fine_row(g, r, live, follow):
        ones = jnp.broadcast_to(live, (HEAD_DIM, live.shape[1]))
        parts = []
        for pair in range(PAIRS):
            weights = weigh(pair)
            rows = value_ref[pair * 2 * HEAD_DIM : (pair + 1) * 2 * HEAD_DIM]
            if pair + 1 < PAIRS:
                score(pair + 1)
            else:
                follow()
            parts += mix_pair(weights, rows, ones)
        start = pl.multiple_of(r * BLOCK, BLOCK)
        mix_ref[g % 2, :, pl.ds(start, BLOCK)] = jnp.concatenate(parts, axis=0).astype(BF16)

    def finish(g):
        out = out_stage(input_ref[g % 2], mix_ref[g % 2], wo_ref, gain_ref)
        fine_ref[g * BAND : (g + 1) * BAND] = out.reshape(BAND, BLOCK, feat)

    arrive(0)
    queries_of(0)
    picks, live = picked(0)
    open_row(0, 0, picks, live)
    for g in range(bands):
        tick((g + 1, 2), (g + 2, 1), (g + LEAD + 2, 0))

        def inner(r, carry, g=g, picks=picks, live=live):
            fine_row(g, r, live, lambda: open_row(g, r + 1, picks, live))
            return carry

        lax.fori_loop(0, BAND - 1, inner, 0)
        last = live
        if g > 0:
            finish(g - 1)
        if g + 1 < bands:
            arrive(g + 1)
            picks, live = picked(g + 1)
            queries_of(g + 1)
        fine_row(
            g,
            BAND - 1,
            last,
            lambda: open_row(g + 1, 0, picks, live) if g + 1 < bands else None,
        )
    finish(bands - 1)

    for g in range(bands):
        for hop in range(len(hops)):
            fine_copy(g, hop).wait_send()


def fused_stage(mesh_rows, n, left_fine, right_fine, left_coarse, right_coarse, lists, counts, w):
    rows, cols, feat = left_fine.shape
    bands = rows // BAND
    coarse_rows, coarse_cols, _ = left_coarse.shape
    keys = lists.shape[2] * cols
    fold = np.tile(np.eye(coarse_cols, dtype=np.float32), (1, HEADS))
    hop_count = len(gather_hops(n, 0))
    vmem = pl.BlockSpec(memory_space=pltpu.VMEM)
    smem = pl.BlockSpec(memory_space=pltpu.SMEM)
    return pl.pallas_call(
        functools.partial(gather_kernel, n=n, row_devices=mesh_rows),
        out_shape=(
            jax.ShapeDtypeStruct(left_fine.shape, BF16),
            jax.ShapeDtypeStruct(left_coarse.shape, BF16),
        ),
        in_specs=[smem, smem] + [vmem] * 11,
        out_specs=(vmem, vmem),
        scratch_shapes=[pltpu.VMEM((n, BAND, cols, feat), BF16) for _ in range(bands)]
        + [
            pltpu.VMEM((coarse_rows + 2, coarse_cols + 2 * EDGE, feat), BF16),
            pltpu.VMEM((feat, feat), BF16),
            pltpu.VMEM((feat, feat), BF16),
            pltpu.VMEM((keys, 2 * BLOCK), F32),
            pltpu.VMEM((keys, 2 * BLOCK), F32),
            pltpu.VMEM((2, 8, 2 * BLOCK), F32),
            pltpu.VMEM((keys, feat), BF16),
            pltpu.VMEM((feat, keys), BF16),
            pltpu.VMEM((2, BAND * BLOCK, feat), BF16),
            pltpu.VMEM((n,) + right_coarse.shape, BF16),
            pltpu.VMEM((coarse_rows + 2, EDGE, feat), BF16),
            pltpu.VMEM((coarse_rows + 2, EDGE, feat), BF16),
            pltpu.VMEM((coarse_rows + 2, coarse_cols, feat), BF16),
            pltpu.VMEM((2, feat, BAND * BLOCK), BF16),
            pltpu.VMEM((feat, HEADS * BLOCK), BF16),
            pltpu.VMEM((2, feat, BAND * BLOCK), BF16),
            pltpu.SemaphoreType.DMA((n - 1,)),
            pltpu.SemaphoreType.DMA((n - 1,)),
            pltpu.SemaphoreType.DMA((4,)),
            pltpu.SemaphoreType.DMA((4,)),
            pltpu.SemaphoreType.DMA((bands, hop_count)),
            pltpu.SemaphoreType.DMA((bands, hop_count)),
            pltpu.SemaphoreType.DMA((bands,)),
        ],
        compiler_params=pltpu.CompilerParams(collective_id=0, has_side_effects=True),
        name="fused_stage",
    )(
        lists,
        counts,
        left_fine,
        right_fine,
        left_coarse,
        right_coarse,
        jnp.asarray(upsample_matrix(coarse_cols), BF16),
        w["wq"],
        w["wk"],
        w["wv"],
        w["wo"],
        w["gain"],
        jnp.asarray(fold, BF16),
    )


def body(
    left_fine,
    right_fine,
    left_coarse,
    right_coarse,
    candidates,
    counts,
    query_weight,
    key_weight,
    value_weight,
    out_weight,
    norm_gain,
):
    w = {
        "wq": query_weight,
        "wk": key_weight,
        "wv": value_weight,
        "wo": out_weight,
        "gain": norm_gain.reshape(1, -1),
    }
    return fused_stage(
        lax.axis_size("rows"),
        lax.axis_size("cols"),
        left_fine,
        right_fine,
        left_coarse,
        right_coarse,
        candidates,
        counts,
        w,
    )


def solution(mesh):
    return jax.shard_map(
        body,
        mesh=mesh,
        in_specs=(
            P("rows", "cols", None),
            P("rows", "cols", None),
            P("rows", "cols", None),
            P("rows", "cols", None),
            P(None, "rows", None),
            P(None, "rows"),
            P(),
            P(),
            P(),
            P(),
            P(),
        ),
        out_specs=(P("rows", "cols", None), P("rows", "cols", None)),
        check_vma=False,
    )
```
